128 devices in a mesh: circ: 8 (over z, y_lo), mer: 16 (over x, y_hi, core).
Axes of the slice: x: 4, y: 4 (y_hi: 2, y_lo: 2; y = y_hi * 2 + y_lo), z: 4, core: 2. Of those that a mesh axis runs over, the one named last changes fastest.
Arguments:
- adjoint: float32 [6, 16, 4096], P(None, 'circ', 'mer'), may hold values from -6 to 6
- mode_fields: float32 [3, 6, 16, 4096], P(None, None, 'circ'), may hold values from -6 to 6
- node_slot: int32 [4096], replicated, may hold values from 0 to 4095, as said below
- thickness: float32 [16, 4096], P('circ'), may hold values from 0.5 to 1.5
- weld_land: int32 [16, 4096], P('circ'), may hold values 0 or 1
- panel_spans: int32 [8, 16], P('circ'), may hold values from 1 to 768, 4096 in all within a row
- load_factor: float32 [], replicated, may hold values from 0.5 to 1.5
- membrane: float32 [24, 24], replicated, may hold values from -1.25 to 1.25
- bending: float32 [24, 24], replicated, may hold values from -0.4375 to 0.4375
- geometric: float32 [3, 24, 24], replicated, may hold values from -1.25 to 1.25
- stress_map: float32 [3, 24], replicated, may hold values from -1.25 to 1.25
Outputs:
- adjoint_load: float32 [6, 16, 4096], P(None, 'circ', 'mer')
- thickness_grad: float32 [16, 12288], P('circ', 'mer')
The draws below stay inside these ranges and needn't reach their ends.
Inputs may be any that keep to these rules, and one draw needn't show every extreme that they name: A permutation of the node positions; node_slot[j] // 256 equals j modulo 4096 // 256. `panel_spans`: each row sums to 4096 and its largest entry is 768.
All inputs are finite; a program needn't handle non-finite values. No bound on the sum of `weld_land` on one device may be relied on, other than what follows from the above.
Results may differ from the reference program's by a relative error of at most 0.0003.
Values sent between devices are 32-bit elements; how exact they have to be, the bound alone decides.
No kernel may reach another device: no remote copies, remote signals or barrier semaphores. Data moves between devices by JAX's collectives and lax.ppermute only.
A program may use at most 128 MiB of HBM per device.

```python
import math
import jax
import jax.numpy as jnp
import numpy as np
from jax import lax

DOF = 6
CR = 2
MERN = 256
NRING = 16
MT = 4096
MOST = 768
N_CIRC = 8
N_MER = 16


def draw_node_slot(key, part):
    groups = MT // MERN
    positions = jnp.arange(MT, dtype=jnp.int32)
    owners = positions % groups
    within = positions // groups
    keys = jax.random.split(jax.random.fold_in(key, 7), groups)
    orders = jax.vmap(lambda single: jax.random.permutation(single, MERN))(keys).astype(jnp.int32)
    return (owners * MERN + orders[owners, within]).astype(jnp.int32)


def place_ends(result, stream_key, least, high):
    longest = result.shape.index(max(result.shape))
    spots = []
    for shift in (0, 1):
        where = [jax.random.randint(jax.random.fold_in(stream_key, axis), (), 0, length) for axis, length in enumerate(result.shape)]
        where[longest] = (where[longest] + shift) % result.shape[longest]
        spots.append(tuple(where))
    return result.at[spots[0]].set(least).at[spots[1]].set(high)


def steps_of(stream_key, extent, cuts, least, high):
    gain = 1.0
    for position, parts in cuts:
        heights = jax.random.uniform(jax.random.fold_in(jax.random.fold_in(stream_key, 6), position), (parts,), jnp.float32, least / len(cuts), high / len(cuts))
        gain = gain * jnp.repeat(jnp.exp(heights), extent[position] // parts).reshape((-1,) + (1,) * (len(extent) - 1 - position))
    return gain


def split_up(amount, total, reach, lean):
    portions = [(1 << 20) // math.isqrt(standing ** lean) + 1 for standing in range(2, amount + 1)]
    surplus, holding = total - reach - (amount - 1), [1] * (amount - 1)
    while surplus > 0:
        movable = [i for i in range(amount - 1) if holding[i] < reach]
        mass, budget = sum([portions[i] for i in movable]), surplus
        for i in movable:
            more = min(reach - holding[i], max(1, budget * portions[i] // mass), surplus)
            holding[i] = holding[i] + more
            surplus = surplus - more
    return np.array([reach] + holding)


def ragged(key, amount, total, limit, skew):
    if amount == 2:
        one = jax.random.randint(key, (), max(1, total - limit), min(limit, total - 1) + 1)
        return jnp.stack([one, total - one])
    tallies = jnp.asarray(split_up(amount, total, limit, skew), jnp.int32)
    twos = (amount - 1) // 2
    source_of, sink = tallies[1:1 + 2 * twos:2], tallies[2:2 + 2 * twos:2]
    slack = jnp.minimum(source_of - 1, limit - sink)
    passed = jax.random.randint(jax.random.fold_in(key, 1), (twos,), 0, 1 << 20) % (slack + 1)
    tallies = tallies.at[1:1 + 2 * twos:2].set(source_of - passed).at[2:2 + 2 * twos:2].set(sink + passed)
    return tallies[jax.random.permutation(jax.random.fold_in(key, 2), amount)]


def noise(key, dims, spread, limit, cuts=(), kind=jnp.bfloat16):
    result = spread * jax.random.normal(key, dims, jnp.float32)
    if cuts:
        result = result * steps_of(key, dims, cuts, -0.22, 0.18)
    return jnp.clip(result, -limit, limit).astype(kind)


def setup_inputs(seed: int = 0) -> dict:
    streams_of = jax.random.split(jax.random.key(seed), 12)
    adjoint = noise(streams_of[0], (DOF, NRING, MT), 1.0, 6.0, ((1, 8), (2, 16)), jnp.float32)
    mode_fields = noise(streams_of[1], (3, DOF, NRING, MT), 1.0, 6.0, ((2, 8),), jnp.float32)
    node_slot = draw_node_slot(jax.random.fold_in(streams_of[11], 71), 0)
    thickness = jnp.clip(jnp.exp(math.log(1.5) - 1.0986123 * jax.random.uniform(streams_of[3], (NRING, MT), jnp.float32) ** steps_of(streams_of[3], (NRING, MT), ((0, 8),), -0.2, 0.2)), 0.5, 1.5)
    weld_land = place_ends((jax.random.randint(streams_of[4], (NRING, MT), 0, 4) < 1).astype(jnp.int32), jax.random.fold_in(streams_of[4], 1), 0, 1)
    panel_spans = jax.vmap(lambda own: ragged(own, N_MER, MT, MOST, 2))(jax.random.split(streams_of[5], N_CIRC)).reshape((N_CIRC, N_MER)).astype(jnp.int32)
    load_factor = jnp.clip(jax.random.uniform(streams_of[6], (), jnp.float32, 0.5, 1.5), 0.5, 1.5)
    membrane = noise(streams_of[7], (24, 24), 24 ** -0.5, 1.25, (), jnp.float32)
    bending = noise(streams_of[8], (24, 24), 216 ** -0.5, 0.4375, (), jnp.float32)
    geometric = noise(streams_of[9], (3, 24, 24), 24 ** -0.5, 1.25, (), jnp.float32)
    stress_map = noise(streams_of[10], (3, 24), 24 ** -0.5, 1.25, (), jnp.float32)
    return dict(adjoint=adjoint, mode_fields=mode_fields, node_slot=node_slot, thickness=thickness, weld_land=weld_land, panel_spans=panel_spans, load_factor=load_factor, membrane=membrane, bending=bending, geometric=geometric, stress_map=stress_map)


highest = lax.Precision.HIGHEST


def element_terms(mode_vectors, adjoint_vectors, thick_rows, weld_rows, load_factor, membrane, bending, geometric, stress_map):
    land_growth = 1.0 + 0.5 * weld_rows
    thick_eff = thick_rows * land_growth
    membrane_part = jnp.einsum("ab,fbe->fae", membrane, mode_vectors, precision=highest)
    bending_part = jnp.einsum("ab,fbe->fae", bending, mode_vectors, precision=highest)
    tangent = membrane_part + 3.0 * thick_eff ** 2 * bending_part
    stiffness = jnp.sum(mode_vectors[0] * tangent[0] + mode_vectors[1] * tangent[1], axis=0)
    adjoint_term = jnp.sum(adjoint_vectors * tangent[2], axis=0)
    stress = jnp.dot(stress_map, mode_vectors[2], precision=highest)
    geometric_part = jnp.einsum("sab,kbe->ksae", geometric, mode_vectors[:2], precision=highest)
    pair_terms = jnp.sum(mode_vectors[:2, None] * geometric_part, axis=(0, 2))
    gradient = land_growth * (stiffness - load_factor * jnp.sum(stress * pair_terms, axis=0) - adjoint_term)
    load_rows = load_factor * thick_eff * jnp.dot(stress_map.T, pair_terms, precision=highest)
    return gradient, load_rows


def corners(field, cycle_axis, cycle_index, slot_here, slot_next):
    lower_cycle = lax.dynamic_index_in_dim(field, cycle_index, cycle_axis, keepdims=False)
    upper_cycle = lax.dynamic_index_in_dim(field, (cycle_index + 1) % NRING, cycle_axis, keepdims=False)
    corner_list = [jnp.take(lower_cycle, slot_here, axis=-1), jnp.take(upper_cycle, slot_here, axis=-1),
                   jnp.take(upper_cycle, slot_next, axis=-1), jnp.take(lower_cycle, slot_next, axis=-1)]
    return jnp.stack(corner_list, axis=-3)


def reference(adjoint, mode_fields, node_slot, thickness, weld_land, panel_spans, load_factor, membrane, bending, geometric, stress_map):
    slot_next = jnp.roll(node_slot, -1)

    def visit_cycle(accumulated, cycle_index):
        mode_vectors = corners(mode_fields, 2, cycle_index, node_slot, slot_next).reshape(3, 24, MT)
        adjoint_vectors = corners(adjoint, 1, cycle_index, node_slot, slot_next).reshape(24, MT)
        thick_rows = lax.dynamic_index_in_dim(thickness, cycle_index, 0, keepdims=False)
        weld_rows = lax.dynamic_index_in_dim(weld_land, cycle_index, 0, keepdims=False).astype(jnp.float32)
        gradient, load_rows = element_terms(mode_vectors, adjoint_vectors, thick_rows, weld_rows, load_factor, membrane, bending, geometric, stress_map)
        load_rows = load_rows.reshape(4, 6, MT)
        next_cycle = (cycle_index + 1) % NRING
        accumulated = accumulated.at[:, cycle_index, node_slot].add(load_rows[0])
        accumulated = accumulated.at[:, next_cycle, node_slot].add(load_rows[1])
        accumulated = accumulated.at[:, next_cycle, slot_next].add(load_rows[2])
        accumulated = accumulated.at[:, cycle_index, slot_next].add(load_rows[3])
        return accumulated, gradient

    adjoint_load, gradient_full = lax.scan(visit_cycle, jnp.zeros((6, NRING, MT), jnp.float32), jnp.arange(NRING, dtype=jnp.int32))
    span_ends = jnp.cumsum(panel_spans, axis=1).astype(jnp.int32)
    span_starts = (span_ends - panel_spans).astype(jnp.int32)
    positions = jnp.arange(MOST, dtype=jnp.int32)
    validity = positions[None, None, :] < panel_spans[:, :, None]
    columns = jnp.where(validity, span_starts[:, :, None] + positions[None, None, :], 0).astype(jnp.int32)
    panels = gradient_full.reshape(N_CIRC, CR, MT)

    def pick_panel(panel_rows, panel_columns):
        return jnp.take(panel_rows, panel_columns.reshape(-1), axis=1).reshape(CR, N_MER, MOST)

    picked = jax.vmap(pick_panel)(panels, columns)
    picked = picked * validity[:, None, :, :].astype(jnp.float32)
    thickness_grad = picked.reshape(NRING, N_MER * MOST)
    return adjoint_load, thickness_grad
```

```python
import jax
import jax.numpy as jnp
from jax import lax
from jax.experimental import pallas as pl
from jax.experimental.pallas import tpu as pltpu
from jax.sharding import PartitionSpec as P

DOF = 6
PAD = 8
OWN = 256
GROUPS = 16
COLUMN = OWN * GROUPS
MOST = 768
LANES = 128
ROWS = COLUMN // LANES
WINDOW = 128
SPREAD = 1024

f32, bf16, i32 = jnp.float32, jnp.bfloat16, jnp.int32
vmem = pl.BlockSpec(memory_space=pltpu.VMEM)
smem = pl.BlockSpec(memory_space=pltpu.SMEM)
raw = pl.BlockSpec(memory_space=pl.ANY)


def iota(shape, axis):
    return lax.broadcasted_iota(i32, shape, axis)


def parts(x):
    high = x.astype(bf16)
    rest = x - high.astype(f32)
    middle = rest.astype(bf16)
    low = (rest - middle.astype(f32)).astype(bf16)
    return high, middle, low


def matmul(a, b):
    return jnp.dot(a, b, preferred_element_type=f32)


def matmul_nt(a, b):
    return lax.dot_general(a, b, (((1,), (1,)), ((), ())), preferred_element_type=f32)


def left_stack(three, axis):
    high, middle, low = three
    return jnp.concatenate([high, high, middle, middle, high, low], axis=axis)


def right_stack(three, axis):
    high, middle, low = three
    return jnp.concatenate([high, middle, high, middle, low, high], axis=axis)


def gather_kernel(modes, adjoint, own, own_adjoint, rim, held, sems):
    member = lax.axis_index("mer")
    copies = []
    for d in range(3):
        block = (member + (d + GROUPS - 1)) & (GROUPS - 1)
        columns = pl.ds(pl.multiple_of(block * OWN, OWN), OWN)
        copies.append(pltpu.make_async_copy(modes.at[:, :, :, columns], held.at[d], sems.at[d]))
        copies[-1].start()
    own[...] = jnp.zeros_like(own)
    own_adjoint[...] = jnp.zeros_like(own_adjoint)
    rim[...] = jnp.zeros_like(rim)
    for i in range(DOF):
        pair = adjoint[i]
        rim[9 * PAD + i : 9 * PAD + i + 1, :] = pair[0:1]
        own_adjoint[i : i + 1, :] = pair[0:1]
        own_adjoint[PAD + i : PAD + i + 1, :] = pair[1:2]
    for d in range(3):
        copies[d].wait()
        for f in range(3):
            for i in range(DOF):
                pair = held[d, f, i]
                rim[(3 * d + f) * PAD + i : (3 * d + f) * PAD + i + 1, :] = pair[0:1]
                own[d, f * PAD + i : f * PAD + i + 1, :] = pair[0:1]
                own[d, (3 + f) * PAD + i : (3 + f) * PAD + i + 1, :] = pair[1:2]


def element_kernel(
    own,
    own_adjoint,
    rim,
    slots,
    thickness,
    weld,
    spans,
    factor,
    membrane,
    bending,
    geometric,
    stress_map,
    sent,
    loads,
    carry,
    thick_rows,
    weld_rows,
    nodes,
):
    member = lax.axis_index("mer")
    load_factor = factor[0]

    lane = iota((1, OWN), 1)
    position = [(lane * GROUPS + (member + d - 1)) & (COLUMN - 1) for d in range(3)]
    pick = [
        (iota((LANES, OWN), 0) == (position[d] & (LANES - 1))).astype(f32).astype(bf16)
        for d in range(3)
    ]
    for a in range(ROWS):
        thick_rows[2 * a : 2 * a + 2, :] = thickness[:, a * LANES : (a + 1) * LANES]
        weld_rows[2 * a : 2 * a + 2, :] = weld[:, a * LANES : (a + 1) * LANES]
    thick_parts = parts(thick_rows[...])
    weld_part = weld_rows[...].astype(f32).astype(bf16)
    slot_part = (slots[...] & (OWN - 1)).astype(f32).astype(bf16)

    def choose(rows, d, stride, offset):
        return jnp.sum(
            jnp.where(
                iota(rows.shape, 0) == (position[d] >> 7) * stride + offset,
                rows,
                0.0,
            ),
            axis=0,
            keepdims=True,
        )

    growth, thick = {}, {}
    stacked = jnp.concatenate([*thick_parts, weld_part], axis=0)
    for d in range(2):
        rows = matmul(stacked, pick[d])
        thick_all = (rows[0:64] + rows[64:128]) + rows[128:192]
        for r in range(2):
            growth[d, r] = 1.0 + 0.5 * choose(rows[192:256], d, 2, r)
            thick[d, r] = choose(thick_all, d, 2, r) * growth[d, r]
    order = []
    for d in range(3):
        slot = choose(matmul(slot_part, pick[d]), d, 1, 0).astype(i32)
        order.append((iota((OWN, OWN), 0) == slot).astype(f32).astype(bf16))

    for d in range(3):
        pieces = [own[d], rim[3 * d * PAD : 3 * (d + 1) * PAD, :]]
        if d == 1:
            pieces += [own_adjoint[...], rim[9 * PAD : 10 * PAD, :]]
        values = jnp.concatenate(pieces, axis=0)
        count = values.shape[0]
        placed = matmul(jnp.concatenate(parts(values), axis=0), order[d])
        for p in range(3):
            nodes[d, p, 0:count, :] = placed[p * count : (p + 1) * count]

    spread = (
        iota((24, 32), 1) == (iota((24, 32), 0) // 6) * PAD + iota((24, 32), 0) % 6
    ).astype(f32).astype(bf16)
    spread_t = (
        iota((32, 24), 0) == (iota((32, 24), 1) // 6) * PAD + iota((32, 24), 1) % 6
    ).astype(f32).astype(bf16)
    stress_rows = jnp.concatenate([stress_map[...], jnp.zeros((5, 24), f32)], axis=0)
    matrices = [membrane[...], bending[...], geometric[0], geometric[1], geometric[2]]
    weights = [[], [], []]
    for matrix in matrices:
        for p, part in enumerate(parts(matrix)):
            wide = matmul(part, spread).astype(bf16)
            weights[p].append(matmul(spread_t, wide))
    stress_parts = parts(stress_rows)
    for p, part in enumerate(stress_parts):
        weights[p].append(matmul(part, spread))
        weights[p].append(jnp.zeros((PAD, 32), f32))
    weights = left_stack([jnp.concatenate(w, axis=0).astype(bf16) for w in weights], 1)
    load_weights = left_stack([matmul_nt(spread_t, part).astype(bf16) for part in stress_parts], 1)
    pair_weights = weights[64:160]
    prestate_weights = jnp.concatenate([weights[0:64], weights[160:176]], axis=0)

    def corner_parts(f, d, r):
        low, high = (f + 3 * r) * PAD, (f + 3 * (r + 1)) * PAD
        out = []
        for p in range(3):
            out.append(
                jnp.concatenate(
                    [
                        nodes[d, p, low : low + PAD, :],
                        nodes[d, p, high : high + PAD, :],
                        nodes[d + 1, p, high : high + PAD, :],
                        nodes[d + 1, p, low : low + PAD, :],
                    ],
                    axis=0,
                )
            )
        return out

    def fold(x):
        return (x[0:8] + x[8:16]) + (x[16:24] + x[24:32])

    def column_sum(x):
        return jnp.sum(x, axis=0, keepdims=True)

    adjoint = [
        (nodes[1, 0, g : g + PAD, :] + nodes[1, 1, g : g + PAD, :]) + nodes[1, 2, g : g + PAD, :]
        for g in (72, 80, 88)
    ]
    result = []
    delayed = []
    load_tiles = {}
    for r in range(2):
        for d in (1, 0):
            bend = 3.0 * thick[d, r] * thick[d, r]
            stiff = jnp.zeros((PAD, OWN), f32)
            pairs = [jnp.zeros((PAD, OWN), f32)] * 3
            for f in range(2):
                three = corner_parts(f, d, r)
                value = (three[0] + three[1]) + three[2]
                stack = right_stack([t.astype(bf16) for t in three], 0)
                if d == 1:
                    product = matmul(weights[0:160], stack)
                    stiff = stiff + fold(value * (product[0:32] + bend * product[32:64]))
                    product = product[64:160]
                else:
                    product = matmul(pair_weights, stack)
                pairs = [
                    pairs[s] + fold(value * product[32 * s : 32 * s + 32]) for s in range(3)
                ]
            pairs = [column_sum(x) for x in pairs]
            three = corner_parts(2, d, r)
            product = matmul(prestate_weights, right_stack([t.astype(bf16) for t in three], 0))
            tangent = product[0:32] + bend * product[32:64]
            if d == 1:
                aterm = column_sum(adjoint[r] * tangent[0:8] + adjoint[r + 1] * tangent[8:16])
                coupling = (
                    product[64:65] * pairs[0] + product[65:66] * pairs[1]
                ) + product[66:67] * pairs[2]
                result.append(
                    growth[d, r] * (column_sum(stiff) - load_factor * coupling - aterm)
                )
            else:
                aterm = column_sum(adjoint[r] * tangent[24:32] + adjoint[r + 1] * tangent[16:24])
                delayed.append(-(growth[d, r] * aterm))
            scale = load_factor * thick[d, r]
            scaled = jnp.concatenate(
                [scale * x for x in pairs] + [jnp.zeros((5, OWN), f32)], axis=0
            )
            load_tiles[d, r] = matmul(load_weights, right_stack(parts(scaled), 0))

    here = [
        load_tiles[1, 0][0:8] + load_tiles[0, 0][24:32],
        (load_tiles[1, 1][0:8] + load_tiles[0, 1][24:32])
        + (load_tiles[1, 0][8:16] + load_tiles[0, 0][16:24]),
        load_tiles[1, 1][8:16] + load_tiles[0, 1][16:24],
    ]
    stored = matmul_nt(jnp.concatenate(parts(jnp.concatenate(here, axis=0)), axis=0), order[1])
    stored = (stored[0:24] + stored[24:48]) + stored[48:72]
    loads[...] = stored[0:16]
    carry[...] = stored[16:24]

    outgoing = jnp.concatenate(result + delayed + [jnp.zeros((4, OWN), f32)], axis=0)
    start = jnp.int32(0)
    for target in range(GROUPS):
        first = (start >> 4) & (OWN - 1)
        turned = pltpu.roll(outgoing, (OWN - first) & (OWN - 1), 1)
        sent[target] = turned[:, 0:WINDOW]
        start = start + spans[0, target]


def span_kernel(received, loads, carry, spans, adjoint_load, thickness_grad):
    member = lax.axis_index("mer")
    start = jnp.int32(0)
    for target in range(GROUPS):
        start = start + jnp.where(target < member, spans[0, target], 0)
    count = spans[0, member]
    offset = start & (GROUPS - 1)

    values = received[...].reshape(GROUPS * PAD, WINDOW)
    expand = (iota((WINDOW, SPREAD), 0) == (iota((WINDOW, SPREAD), 1) >> 4)).astype(f32).astype(bf16)
    rows = matmul(jnp.concatenate(parts(values), axis=0), expand)
    n = GROUPS * PAD
    rows = (rows[0:n] + rows[n : 2 * n]) + rows[2 * n : 3 * n]
    residue = iota((PAD, SPREAD), 1) & (GROUPS - 1)
    sequence = jnp.zeros((PAD, SPREAD), f32)
    for g in range(GROUPS):
        sequence = jnp.where(residue == g, rows[g * PAD : (g + 1) * PAD], sequence)
    now = pltpu.roll(sequence, (SPREAD - offset) & (SPREAD - 1), 1)
    late = pltpu.roll(sequence, (SPREAD - 1 - offset) & (SPREAD - 1), 1)
    gradient = now[0:2, 0:MOST] + late[2:4, 0:MOST]
    thickness_grad[...] = jnp.where(iota((2, MOST), 1) < count, gradient, 0.0)

    first = loads[0:PAD] + carry[...]
    second = loads[PAD : 2 * PAD]
    for i in range(DOF):
        adjoint_load[i, 0:1, :] = first[i : i + 1]
        adjoint_load[i, 1:2, :] = second[i : i + 1]


def shape(*dims):
    return jax.ShapeDtypeStruct(dims, f32)


def from_behind(block, axis, distance):
    size = lax.axis_size(axis)
    return lax.ppermute(block, axis, [((i - distance) % size, i) for i in range(size)])


def on_device(
    adjoint,
    mode_fields,
    node_slot,
    thickness,
    weld_land,
    panel_spans,
    load_factor,
    membrane,
    bending,
    geometric,
    stress_map,
):
    own, own_adjoint, rim = pl.pallas_call(
        gather_kernel,
        out_shape=(shape(3, 6 * PAD, OWN), shape(2 * PAD, OWN), shape(10 * PAD, OWN)),
        in_specs=[raw, vmem],
        out_specs=(vmem, vmem, vmem),
        scratch_shapes=[pltpu.VMEM((3, 3, DOF, 2, OWN), f32), pltpu.SemaphoreType.DMA((3,))],
    )(mode_fields, adjoint)
    rim = from_behind(rim, "circ", -1)
    sent, loads, carry = pl.pallas_call(
        element_kernel,
        out_shape=(shape(GROUPS, PAD, WINDOW), shape(2 * PAD, OWN), shape(PAD, OWN)),
        in_specs=[vmem] * 6 + [smem, smem] + [vmem] * 4,
        out_specs=(vmem, vmem, vmem),
        scratch_shapes=[
            pltpu.VMEM((2 * ROWS, LANES), f32),
            pltpu.VMEM((2 * ROWS, LANES), i32),
            pltpu.VMEM((3, 3, 12 * PAD, OWN), f32),
        ],
    )(
        own,
        own_adjoint,
        rim,
        node_slot.reshape(ROWS, LANES),
        thickness,
        weld_land,
        panel_spans,
        load_factor.reshape(1),
        membrane,
        bending,
        geometric,
        stress_map,
    )
    carry = from_behind(carry, "circ", 1)
    received = lax.all_to_all(sent, "mer", 0, 0)
    return pl.pallas_call(
        span_kernel,
        out_shape=(shape(DOF, 2, OWN), shape(2, MOST)),
        in_specs=[vmem] * 3 + [smem],
        out_specs=(vmem, vmem),
    )(received, loads, carry, panel_spans)


def solution(mesh):
    return jax.shard_map(
        on_device,
        mesh=mesh,
        in_specs=(
            P(None, "circ", "mer"),
            P(None, None, "circ", None),
            P(),
            P("circ", None),
            P("circ", None),
            P("circ", None),
            P(),
            P(),
            P(),
            P(),
            P(),
        ),
        out_specs=(P(None, "circ", "mer"), P("circ", "mer")),
        check_vma=False,
    )
```

```python
import jax
import jax.numpy as jnp
from jax import lax
from jax.experimental import pallas as pl
from jax.experimental.pallas import tpu as pltpu
from jax.sharding import PartitionSpec as P


DOF = 6
SMALL = 8
PAD = 8
OWN = 256
GROUPS = 16
COLUMN = OWN * GROUPS
MOST = 768
LANES = 128
ROWS = COLUMN // LANES
WINDOW = 128
HALF = 64

f32, bf16, i32 = jnp.float32, jnp.bfloat16, jnp.int32
vmem = pl.BlockSpec(memory_space=pltpu.VMEM)
smem = pl.BlockSpec(memory_space=pltpu.SMEM)
hbm = pl.BlockSpec(memory_space=pltpu.HBM)
small = pltpu.CompilerParams(vmem_limit_bytes=12 << 20)


def iota(shape, axis):
    return lax.broadcasted_iota(i32, shape, axis)


def parts(x):
    high = x.astype(bf16)
    rest = x - high.astype(f32)
    middle = rest.astype(bf16)
    low = (rest - middle.astype(f32)).astype(bf16)
    return high, middle, low


def matmul(a, b):
    return jnp.dot(a, b, preferred_element_type=f32)


def matmul_nt(a, b):
    return lax.dot_general(a, b, (((1,), (1,)), ((), ())), preferred_element_type=f32)


def left_stack(three, axis):
    high, middle, low = three
    return jnp.concatenate([high, high, middle, middle, high, low], axis=axis)


def right_stack(three, axis):
    high, middle, low = three
    return jnp.concatenate([high, middle, high, middle, low, high], axis=axis)


def gather_kernel(modes, adjoint, *rest):
    small_in, rest = rest[:SMALL], rest[SMALL:]
    own, own_adjoint, rim, *rest = rest
    small_out, (held, held_adjoint, sems) = rest[:SMALL], rest[SMALL:]
    member = lax.axis_index("mer")
    copies = []
    for d in range(3):
        block = (member + (d + GROUPS - 1)) & (GROUPS - 1)
        columns = pl.ds(pl.multiple_of(block * OWN, OWN), OWN)
        copies.append(pltpu.make_async_copy(modes.at[:, :, :, columns], held.at[d], sems.at[d]))
    copies.append(pltpu.make_async_copy(adjoint, held_adjoint, sems.at[3]))
    for i in range(SMALL):
        copies.append(pltpu.make_async_copy(small_in[i], small_out[i], sems.at[4 + i]))
    for copy in copies:
        copy.start()
    own[...] = jnp.zeros_like(own)
    own_adjoint[...] = jnp.zeros_like(own_adjoint)
    rim[...] = jnp.zeros_like(rim)
    for d in range(3):
        copies[d].wait()
        for f in range(3):
            for i in range(DOF):
                pair = held[d, f, i]
                rim[(3 * d + f) * PAD + i : (3 * d + f) * PAD + i + 1, :] = pair[0:1]
                own[d, f * PAD + i : f * PAD + i + 1, :] = pair[0:1]
                own[d, (3 + f) * PAD + i : (3 + f) * PAD + i + 1, :] = pair[1:2]
    for copy in copies[3:]:
        copy.wait()
    for i in range(DOF):
        pair = held_adjoint[i]
        rim[9 * PAD + i : 9 * PAD + i + 1, :] = pair[0:1]
        own_adjoint[i : i + 1, :] = pair[0:1]
        own_adjoint[PAD + i : PAD + i + 1, :] = pair[1:2]


def fold(x):
    return (x[0:8] + x[8:16]) + (x[16:24] + x[24:32])


def column_sum(x):
    return jnp.sum(x, axis=0, keepdims=True)


def cycle_terms(corner_parts, adjoint, growth, thick, weights):
    bend = [3.0 * t * t for t in thick]
    pair_weights = weights[64:160]
    prestate_weights = jnp.concatenate([weights[0:64], weights[160:176]], axis=0)
    outcome = {}
    for d in (1, 0):
        stiff = jnp.zeros((PAD, OWN), f32)
        pairs = [jnp.zeros((PAD, OWN), f32)] * 3
        for f in range(2):
            three = corner_parts(f, d)
            value = (three[0] + three[1]) + three[2]
            stack = right_stack([t.astype(bf16) for t in three], 0)
            if d == 1:
                product = matmul(weights[0:160], stack)
                stiff = stiff + fold(value * (product[0:32] + bend[d] * product[32:64]))
                product = product[64:160]
            else:
                product = matmul(pair_weights, stack)
            pairs = [pairs[s] + fold(value * product[32 * s : 32 * s + 32]) for s in range(3)]
        pairs = [column_sum(x) for x in pairs]
        stack = right_stack([t.astype(bf16) for t in corner_parts(2, d)], 0)
        product = matmul(prestate_weights, stack)
        tangent = product[0:32] + bend[d] * product[32:64]
        if d == 1:
            aterm = column_sum(adjoint[0] * tangent[0:8] + adjoint[1] * tangent[8:16])
            coupling = (
                product[64:65] * pairs[0] + product[65:66] * pairs[1]
            ) + product[66:67] * pairs[2]
            rows = [growth[d] * (column_sum(stiff) - aterm), growth[d] * coupling]
        else:
            aterm = column_sum(adjoint[0] * tangent[24:32] + adjoint[1] * tangent[16:24])
            rows.append(-(growth[d] * aterm))
        outcome[d] = [thick[d] * x for x in pairs] + [jnp.zeros((5, OWN), f32)]
    return rows, jnp.concatenate(outcome[0] + outcome[1], axis=0)


def corner_rows():
    entry = iota((32, 24), 1)
    return (iota((32, 24), 0) == (entry // 6) * PAD + entry % 6).astype(f32).astype(bf16)


def stored_order(rows, order):
    n = rows.shape[0]
    placed = matmul_nt(jnp.concatenate(parts(rows), axis=0), order)
    return (placed[0:n] + placed[n : 2 * n]) + placed[2 * n : 3 * n]


def local_kernel(
    own,
    own_adjoint,
    slots,
    thickness,
    weld,
    membrane,
    bending,
    geometric,
    stress_map,
    order,
    second,
    second_adjoint,
    weights,
    scalings,
    gradients,
    pairs,
    thick_rows,
    weld_rows,
    nodes,
):
    member = lax.axis_index("mer")

    lane = iota((1, OWN), 1)
    position = [(lane * GROUPS + (member + d - 1)) & (COLUMN - 1) for d in range(3)]
    pick = [
        (iota((LANES, OWN), 0) == (position[d] & (LANES - 1))).astype(f32).astype(bf16)
        for d in range(3)
    ]
    for a in range(ROWS):
        thick_rows[2 * a : 2 * a + 2, :] = thickness[:, a * LANES : (a + 1) * LANES]
        weld_rows[2 * a : 2 * a + 2, :] = weld[:, a * LANES : (a + 1) * LANES]
    thick_parts = parts(thick_rows[...])
    weld_part = weld_rows[...].astype(f32).astype(bf16)
    slot_part = (slots[...] & (OWN - 1)).astype(f32).astype(bf16)

    def choose(rows, d, stride, offset):
        here = iota(rows.shape, 0) == (position[d] >> 7) * stride + offset
        return column_sum(jnp.where(here, rows, 0.0))

    growth, thick = {}, {}
    stacked = jnp.concatenate([*thick_parts, weld_part], axis=0)
    for d in range(2):
        rows = matmul(stacked, pick[d])
        thick_all = (rows[0:64] + rows[64:128]) + rows[128:192]
        for r in range(2):
            growth[d, r] = 1.0 + 0.5 * choose(rows[192:256], d, 2, r)
            thick[d, r] = choose(thick_all, d, 2, r) * growth[d, r]
    scalings[...] = jnp.concatenate(
        [growth[0, 1], growth[1, 1], thick[0, 1], thick[1, 1], jnp.zeros((4, OWN), f32)], axis=0
    )

    for d in range(3):
        slot = choose(matmul(slot_part, pick[d]), d, 1, 0).astype(i32)
        order[d] = (iota((OWN, OWN), 0) == slot).astype(f32).astype(bf16)
        values = own[d]
        if d == 1:
            values = jnp.concatenate([values, own_adjoint[...]], axis=0)
        count = values.shape[0]
        placed = matmul(jnp.concatenate(parts(values), axis=0), order[d])
        for p in range(3):
            nodes[d, p, 0:count, :] = placed[p * count : (p + 1) * count]
            second[d, p] = placed[p * count + 24 : p * count + 48]

    spread = (
        iota((24, 32), 1) == (iota((24, 32), 0) // 6) * PAD + iota((24, 32), 0) % 6
    ).astype(f32).astype(bf16)
    spread_t = corner_rows()
    stress_rows = jnp.concatenate([stress_map[...], jnp.zeros((5, 24), f32)], axis=0)
    matrices = [membrane[...], bending[...], geometric[0], geometric[1], geometric[2]]
    pieces = [[], [], []]
    for matrix in matrices:
        for p, part in enumerate(parts(matrix)):
            wide = matmul(part, spread).astype(bf16)
            pieces[p].append(matmul(spread_t, wide))
    for p, part in enumerate(parts(stress_rows)):
        pieces[p].append(matmul(part, spread))
        pieces[p].append(jnp.zeros((PAD, 32), f32))
    weights[...] = left_stack([jnp.concatenate(w, axis=0).astype(bf16) for w in pieces], 1)

    def corner_parts(f, d):
        low, high = f * PAD, (f + 3) * PAD
        return [
            jnp.concatenate(
                [
                    nodes[d, p, low : low + PAD, :],
                    nodes[d, p, high : high + PAD, :],
                    nodes[d + 1, p, high : high + PAD, :],
                    nodes[d + 1, p, low : low + PAD, :],
                ],
                axis=0,
            )
            for p in range(3)
        ]

    adjoint = [
        (nodes[1, 0, g : g + PAD, :] + nodes[1, 1, g : g + PAD, :]) + nodes[1, 2, g : g + PAD, :]
        for g in (48, 56)
    ]
    second_adjoint[...] = adjoint[1]
    rows, pair_rows = cycle_terms(
        corner_parts,
        adjoint,
        [growth[d, 0] for d in range(2)],
        [thick[d, 0] for d in range(2)],
        weights[...],
    )
    gradients[...] = jnp.concatenate(rows + [jnp.zeros((5, OWN), f32)], axis=0)
    pairs[...] = pair_rows


def rim_kernel(
    rim,
    order,
    second,
    second_adjoint,
    weights,
    scalings,
    gradients,
    spans,
    sent,
    pairs,
    nodes,
    counts,
    sem,
):
    fetch = pltpu.make_async_copy(spans, counts, sem)
    fetch.start()
    for d in range(3):
        values = rim[3 * d * PAD : 3 * (d + 1) * PAD, :]
        if d == 1:
            values = jnp.concatenate([values, rim[9 * PAD : 10 * PAD, :]], axis=0)
        count = values.shape[0]
        placed = matmul(jnp.concatenate(parts(values), axis=0), order[d])
        for p in range(3):
            nodes[d, p, 0:count, :] = placed[p * count : (p + 1) * count]

    def corner_parts(f, d):
        rows = slice(f * PAD, (f + 1) * PAD)
        return [
            jnp.concatenate(
                [
                    second[d, p, rows, :],
                    nodes[d, p, rows, :],
                    nodes[d + 1, p, rows, :],
                    second[d + 1, p, rows, :],
                ],
                axis=0,
            )
            for p in range(3)
        ]

    adjoint = [second_adjoint[...], (nodes[1, 0, 24:32, :] + nodes[1, 1, 24:32, :]) + nodes[1, 2, 24:32, :]]
    rows, pair_rows = cycle_terms(
        corner_parts,
        adjoint,
        [scalings[0:1, :], scalings[1:2, :]],
        [scalings[2:3, :], scalings[3:4, :]],
        weights[...],
    )
    pairs[...] = pair_rows

    odd = (lax.axis_index("mer") & 1) == 1
    none = jnp.zeros((1, OWN), f32)

    def four_of_eight(four):
        return jnp.concatenate(
            [jnp.where(odd, 0.0, x) for x in four] + [jnp.where(odd, x, 0.0) for x in four], axis=0
        )

    now = four_of_eight([gradients[0:1, :], rows[0], gradients[1:2, :], rows[1]])
    late = four_of_eight([gradients[2:3, :], rows[2], none, none])
    lower = iota((PAD, WINDOW), 1) < HALF
    fetch.wait()
    start = jnp.int32(0)
    for target in range(GROUPS):
        first = (start >> 4) & (OWN - 1)
        turned = pltpu.roll(now, (OWN - first) & (OWN - 1), 1)
        turned_late = pltpu.roll(late, (OWN + HALF - first) & (OWN - 1), 1)
        sent[target] = jnp.where(lower, turned[:, 0:WINDOW], turned_late[:, 0:WINDOW])
        start = start + counts[0, target]


def load_kernel(first_pairs, second_pairs, order, stress_map, factor, loads, carry):
    stress_rows = jnp.concatenate([stress_map[...], jnp.zeros((5, 24), f32)], axis=0)
    spread_t = corner_rows()
    load_weights = left_stack([matmul_nt(spread_t, part).astype(bf16) for part in parts(stress_rows)], 1)
    lower, upper = [], []
    for pairs in (first_pairs, second_pairs):
        before = matmul(load_weights, right_stack(parts(pairs[0:PAD, :]), 0))
        here = matmul(load_weights, right_stack(parts(pairs[PAD : 2 * PAD, :]), 0))
        lower.append(here[0:8] + before[24:32])
        upper.append(here[8:16] + before[16:24])
    stored = stored_order(jnp.concatenate([lower[0], upper[0] + lower[1], upper[1]], axis=0), order[1])
    stored = factor[0] * stored
    loads[...] = stored[0 : 2 * PAD]
    carry[...] = stored[2 * PAD : 3 * PAD]


def place_kernel(spans, spread_now, spread_late, sources):
    member = lax.axis_index("mer")
    group = iota((1, GROUPS), 1)
    start = jnp.sum(jnp.where(group < member, spans[...], 0), axis=1, keepdims=True)
    count = jnp.sum(jnp.where(group == member, spans[...], 0), axis=1, keepdims=True)
    element = iota((1, MOST), 1) + (start & (GROUPS - 1))
    valid = iota((1, MOST), 1) < count
    for late, spread_ref in ((0, spread_now), (1, spread_late)):
        sources[late : late + 1, :] = jnp.where(valid, (element + late) & (GROUPS - 1), -1)
        third = (iota((HALF, MOST), 0) == ((element + late) >> 4)).astype(f32).astype(bf16)
        for p in range(3):
            spread_ref[p * HALF : (p + 1) * HALF, :] = third


def span_kernel(received, loads, carry, spread_now, spread_late, sources, factor, adjoint_load, thickness_grad):
    values = jnp.concatenate([received[2 * g] + received[2 * g + 1] for g in range(GROUPS // 2)], axis=0)
    lower_half = iota((PAD, MOST), 0) < 4
    both = []
    for late, spread_ref in ((0, spread_now), (1, spread_late)):
        stack = jnp.concatenate(parts(values[:, late * HALF : (late + 1) * HALF]), axis=1)
        rows = matmul(stack, spread_ref[...])
        source = sources[late : late + 1, :]
        wanted = jnp.where(lower_half, source, source - 1)
        picked = jnp.zeros((PAD, MOST), f32)
        for g in range(GROUPS // 2):
            picked = jnp.where(wanted == 2 * g, rows[g * PAD : (g + 1) * PAD], picked)
        both.append(picked[0:4] + picked[4:8])
    thickness_grad[...] = (both[0][0:2] - factor[0] * both[0][2:4]) + both[1][0:2]

    first = loads[0:PAD, :] + carry[...]
    second = loads[PAD : 2 * PAD, :]
    for i in range(DOF):
        adjoint_load[i, 0:1, :] = first[i : i + 1]
        adjoint_load[i, 1:2, :] = second[i : i + 1]


def shape(*dims, dtype=f32):
    return jax.ShapeDtypeStruct(dims, dtype)


def from_behind(block, axis, distance):
    size = lax.axis_size(axis)
    return lax.ppermute(block, axis, [((i - distance) % size, i) for i in range(size)])


def on_device(
    adjoint,
    mode_fields,
    node_slot,
    thickness,
    weld_land,
    panel_spans,
    load_factor,
    membrane,
    bending,
    geometric,
    stress_map,
):
    brought = (node_slot.reshape(ROWS, LANES), thickness, weld_land, membrane, bending, geometric, stress_map, panel_spans)
    own, own_adjoint, rim, *brought = pl.pallas_call(
        gather_kernel,
        out_shape=(shape(3, 6 * PAD, OWN), shape(2 * PAD, OWN), shape(10 * PAD, OWN))
        + tuple(shape(*x.shape, dtype=x.dtype) for x in brought),
        in_specs=[hbm] * (2 + SMALL),
        out_specs=(vmem,) * (3 + SMALL),
        scratch_shapes=[
            pltpu.VMEM((3, 3, DOF, 2, OWN), f32),
            pltpu.VMEM((DOF, 2, OWN), f32),
            pltpu.SemaphoreType.DMA((4 + SMALL,)),
        ],
        compiler_params=small,
    )(*[pltpu.with_memory_space_constraint(x, pltpu.HBM) for x in (mode_fields, adjoint, *brought)])
    *brought, panel_spans = brought
    stress_map = brought[-1]
    rim = from_behind(rim, "circ", -1)
    order, *kept, first_pairs = pl.pallas_call(
        local_kernel,
        out_shape=(
            shape(3, OWN, OWN, dtype=bf16),
            shape(3, 3, 3 * PAD, OWN),
            shape(PAD, OWN),
            shape(176, 192, dtype=bf16),
            shape(PAD, OWN),
            shape(PAD, OWN),
            shape(2 * PAD, OWN),
        ),
        in_specs=[vmem] * 9,
        out_specs=(vmem,) * 7,
        scratch_shapes=[
            pltpu.VMEM((2 * ROWS, LANES), f32),
            pltpu.VMEM((2 * ROWS, LANES), i32),
            pltpu.VMEM((3, 3, 8 * PAD, OWN), f32),
        ],
        compiler_params=small,
    )(own, own_adjoint, *brought)
    sent, second_pairs = pl.pallas_call(
        rim_kernel,
        out_shape=(shape(GROUPS, PAD, WINDOW), shape(2 * PAD, OWN)),
        in_specs=[vmem] * 8,
        out_specs=(vmem,) * 2,
        scratch_shapes=[
            pltpu.VMEM((3, 3, 4 * PAD, OWN), f32),
            pltpu.SMEM((1, GROUPS), i32),
            pltpu.SemaphoreType.DMA,
        ],
        compiler_params=small,
    )(rim, order, *kept, panel_spans)
    received = lax.all_to_all(sent, "mer", 0, 0)
    second_pairs, factor = lax.optimization_barrier((second_pairs, load_factor.reshape(1)))
    loads, carry = pl.pallas_call(
        load_kernel,
        out_shape=(shape(2 * PAD, OWN), shape(PAD, OWN)),
        in_specs=[vmem] * 4 + [smem],
        out_specs=(vmem,) * 2,
        compiler_params=small,
    )(first_pairs, second_pairs, order, stress_map, factor)
    carry = from_behind(carry, "circ", 1)
    places = pl.pallas_call(
        place_kernel,
        out_shape=(shape(3 * HALF, MOST, dtype=bf16), shape(3 * HALF, MOST, dtype=bf16), shape(2, MOST, dtype=i32)),
        in_specs=[vmem],
        out_specs=(vmem,) * 3,
        compiler_params=small,
    )(panel_spans)
    return pl.pallas_call(
        span_kernel,
        out_shape=(shape(DOF, 2, OWN), shape(2, MOST)),
        in_specs=[vmem] * 6 + [smem],
        out_specs=(vmem,) * 2,
        compiler_params=small,
    )(received, loads, carry, *places, factor)


def solution(mesh):
    return jax.shard_map(
        on_device,
        mesh=mesh,
        in_specs=(
            P(None, "circ", "mer"),
            P(None, None, "circ", None),
            P(),
            P("circ", None),
            P("circ", None),
            P("circ", None),
            P(),
            P(),
            P(),
            P(),
            P(),
        ),
        out_specs=(P(None, "circ", "mer"), P("circ", "mer")),
        check_vma=False,
    )
```

```python
import jax
import jax.numpy as jnp
from jax import lax
from jax.experimental import pallas as pl
from jax.experimental.pallas import tpu as pltpu
from jax.sharding import PartitionSpec as P


DOF = 6
SMALL = 2
PAD = 8
OWN = 256
GROUPS = 16
COLUMN = OWN * GROUPS
MOST = 768
LANES = 128
ROWS = COLUMN // LANES
WINDOW = 128
HALF = 64

f32, bf16, i32 = jnp.float32, jnp.bfloat16, jnp.int32
vmem = pl.BlockSpec(memory_space=pltpu.VMEM)
smem = pl.BlockSpec(memory_space=pltpu.SMEM)
hbm = pl.BlockSpec(memory_space=pltpu.HBM)
small = pltpu.CompilerParams(vmem_limit_bytes=12 << 20)


def iota(shape, axis):
    return lax.broadcasted_iota(i32, shape, axis)


def parts(x):
    high = x.astype(bf16)
    rest = x - high.astype(f32)
    middle = rest.astype(bf16)
    low = (rest - middle.astype(f32)).astype(bf16)
    return high, middle, low


def matmul(a, b):
    return jnp.dot(a, b, preferred_element_type=f32)


def matmul_nt(a, b):
    return lax.dot_general(a, b, (((1,), (1,)), ((), ())), preferred_element_type=f32)


def left_stack(three, axis):
    high, middle, low = three
    return jnp.concatenate([high, high, middle, middle, high, low], axis=axis)


def right_stack(three, axis):
    high, middle, low = three
    return jnp.concatenate([high, middle, high, middle, low, high], axis=axis)


def gather_kernel(modes, adjoint, *rest):
    small_in, rest = rest[:SMALL], rest[SMALL:]
    held, held_adjoint, rim, *rest = rest
    small_out, (sems,) = rest[:SMALL], rest[SMALL:]
    member = lax.axis_index("mer")
    copies = []
    for d in range(3):
        block = (member + (d + GROUPS - 1)) & (GROUPS - 1)
        columns = pl.ds(pl.multiple_of(block * OWN, OWN), OWN)
        copies.append(pltpu.make_async_copy(modes.at[:, :, :, columns], held.at[d], sems.at[d]))
    copies.append(pltpu.make_async_copy(adjoint, held_adjoint, sems.at[3]))
    for i in range(SMALL):
        copies.append(pltpu.make_async_copy(small_in[i], small_out[i], sems.at[4 + i]))
    for copy in copies:
        copy.start()
    rim[56:64, :] = jnp.zeros((PAD, OWN), f32)
    for d in range(3):
        copies[d].wait()
        for f in range(3):
            for i in range(DOF):
                row = (3 * d + f) * DOF + i
                rim[row : row + 1, :] = held[d, f, i, 0:1, :]
    for copy in copies[3:]:
        copy.wait()
    for i in range(DOF):
        rim[54 + i : 55 + i, :] = held_adjoint[i, 0:1, :]


def fold(x):
    return (x[0:8] + x[8:16]) + (x[16:24] + x[24:32])


def column_sum(x):
    return jnp.sum(x, axis=0, keepdims=True)


def cycle_terms(corner_parts, adjoint, growth, thick, weights):
    bend = [3.0 * t * t for t in thick]
    pair_weights = weights[64:160]
    prestate_weights = jnp.concatenate([weights[0:64], weights[160:176]], axis=0)
    outcome = {}
    for d in (1, 0):
        stiff = jnp.zeros((PAD, OWN), f32)
        pairs = [jnp.zeros((PAD, OWN), f32)] * 3
        for f in range(2):
            three = corner_parts(f, d)
            value = (three[0] + three[1]) + three[2]
            stack = right_stack([t.astype(bf16) for t in three], 0)
            if d == 1:
                product = matmul(weights[0:160], stack)
                stiff = stiff + fold(value * (product[0:32] + bend[d] * product[32:64]))
                product = product[64:160]
            else:
                product = matmul(pair_weights, stack)
            pairs = [pairs[s] + fold(value * product[32 * s : 32 * s + 32]) for s in range(3)]
        pairs = [column_sum(x) for x in pairs]
        stack = right_stack([t.astype(bf16) for t in corner_parts(2, d)], 0)
        product = matmul(prestate_weights, stack)
        tangent = product[0:32] + bend[d] * product[32:64]
        if d == 1:
            aterm = column_sum(adjoint[0] * tangent[0:8] + adjoint[1] * tangent[8:16])
            coupling = (
                product[64:65] * pairs[0] + product[65:66] * pairs[1]
            ) + product[66:67] * pairs[2]
            rows = [growth[d] * (column_sum(stiff) - aterm), growth[d] * coupling]
        else:
            aterm = column_sum(adjoint[0] * tangent[24:32] + adjoint[1] * tangent[16:24])
            rows.append(-(growth[d] * aterm))
        outcome[d] = [thick[d] * x for x in pairs] + [jnp.zeros((5, OWN), f32)]
    return rows, jnp.concatenate(outcome[0] + outcome[1], axis=0)


def corner_rows():
    entry = iota((32, 24), 1)
    return (iota((32, 24), 0) == (entry // 6) * PAD + entry % 6).astype(f32).astype(bf16)


def stored_order(rows, order):
    n = rows.shape[0]
    placed = matmul_nt(jnp.concatenate(parts(rows), axis=0), order)
    return (placed[0:n] + placed[n : 2 * n]) + placed[2 * n : 3 * n]


def local_kernel(
    held,
    held_adjoint,
    slots,
    thickness,
    weld,
    membrane,
    bending,
    geometric,
    stress_map,
    order,
    second,
    second_adjoint,
    weights,
    scalings,
    gradients,
    pairs,
    thick_rows,
    weld_rows,
    nodes,
    own,
):
    member = lax.axis_index("mer")

    lane = iota((1, OWN), 1)
    position = [(lane * GROUPS + (member + d - 1)) & (COLUMN - 1) for d in range(3)]
    pick = [
        (iota((LANES, OWN), 0) == (position[d] & (LANES - 1))).astype(f32).astype(bf16)
        for d in range(3)
    ]
    for a in range(ROWS):
        thick_rows[2 * a : 2 * a + 2, :] = thickness[:, a * LANES : (a + 1) * LANES]
        weld_rows[2 * a : 2 * a + 2, :] = weld[:, a * LANES : (a + 1) * LANES]
    thick_parts = parts(thick_rows[...])
    weld_part = weld_rows[...].astype(f32).astype(bf16)
    slot_part = (slots[...] & (OWN - 1)).astype(f32).astype(bf16)

    def choose(rows, d, stride, offset):
        here = iota(rows.shape, 0) == (position[d] >> 7) * stride + offset
        return column_sum(jnp.where(here, rows, 0.0))

    growth, thick = {}, {}
    stacked = jnp.concatenate([*thick_parts, weld_part], axis=0)
    for d in range(2):
        rows = matmul(stacked, pick[d])
        thick_all = (rows[0:64] + rows[64:128]) + rows[128:192]
        for r in range(2):
            growth[d, r] = 1.0 + 0.5 * choose(rows[192:256], d, 2, r)
            thick[d, r] = choose(thick_all, d, 2, r) * growth[d, r]
    scalings[...] = jnp.concatenate(
        [growth[0, 1], growth[1, 1], thick[0, 1], thick[1, 1], jnp.zeros((4, OWN), f32)], axis=0
    )

    own[...] = jnp.zeros_like(own)
    for r in range(2):
        for i in range(DOF):
            for d in range(3):
                for f in range(3):
                    row = (f + 3 * r) * PAD + i
                    own[d, row : row + 1, :] = held[d, f, i, r : r + 1, :]
            row = (6 + r) * PAD + i
            own[1, row : row + 1, :] = held_adjoint[i, r : r + 1, :]
    for d in range(3):
        slot = choose(matmul(slot_part, pick[d]), d, 1, 0).astype(i32)
        order[d] = (iota((OWN, OWN), 0) == slot).astype(f32).astype(bf16)
        count = 8 * PAD if d == 1 else 6 * PAD
        values = own[d, 0:count, :]
        placed = matmul(jnp.concatenate(parts(values), axis=0), order[d])
        for p in range(3):
            nodes[d, p, 0:count, :] = placed[p * count : (p + 1) * count]
            second[d, p] = placed[p * count + 24 : p * count + 48]

    spread = (
        iota((24, 32), 1) == (iota((24, 32), 0) // 6) * PAD + iota((24, 32), 0) % 6
    ).astype(f32).astype(bf16)
    spread_t = corner_rows()
    stress_rows = jnp.concatenate([stress_map[...], jnp.zeros((5, 24), f32)], axis=0)
    matrices = [membrane[...], bending[...], geometric[0], geometric[1], geometric[2]]
    pieces = [[], [], []]
    for matrix in matrices:
        for p, part in enumerate(parts(matrix)):
            wide = matmul(part, spread).astype(bf16)
            pieces[p].append(matmul(spread_t, wide))
    for p, part in enumerate(parts(stress_rows)):
        pieces[p].append(matmul(part, spread))
        pieces[p].append(jnp.zeros((PAD, 32), f32))
    weights[...] = left_stack([jnp.concatenate(w, axis=0).astype(bf16) for w in pieces], 1)

    def corner_parts(f, d):
        low, high = f * PAD, (f + 3) * PAD
        return [
            jnp.concatenate(
                [
                    nodes[d, p, low : low + PAD, :],
                    nodes[d, p, high : high + PAD, :],
                    nodes[d + 1, p, high : high + PAD, :],
                    nodes[d + 1, p, low : low + PAD, :],
                ],
                axis=0,
            )
            for p in range(3)
        ]

    adjoint = [
        (nodes[1, 0, g : g + PAD, :] + nodes[1, 1, g : g + PAD, :]) + nodes[1, 2, g : g + PAD, :]
        for g in (48, 56)
    ]
    second_adjoint[...] = adjoint[1]
    rows, pair_rows = cycle_terms(
        corner_parts,
        adjoint,
        [growth[d, 0] for d in range(2)],
        [thick[d, 0] for d in range(2)],
        weights[...],
    )
    gradients[...] = jnp.concatenate(rows + [jnp.zeros((5, OWN), f32)], axis=0)
    pairs[...] = pair_rows


def rim_kernel(
    rim,
    order,
    second,
    second_adjoint,
    weights,
    scalings,
    gradients,
    spans,
    sent,
    pairs,
    nodes,
    counts,
    sem,
):
    fetch = pltpu.make_async_copy(spans, counts, sem)
    fetch.start()
    for d in range(3):
        groups = [3 * d, 3 * d + 1, 3 * d + 2] + [9] * (d == 1)
        values = jnp.concatenate([rim[g * DOF : g * DOF + PAD, :] for g in groups], axis=0)
        count = values.shape[0]
        placed = matmul(jnp.concatenate(parts(values), axis=0), order[d])
        for p in range(3):
            nodes[d, p, 0:count, :] = placed[p * count : (p + 1) * count]

    def corner_parts(f, d):
        rows = slice(f * PAD, (f + 1) * PAD)
        return [
            jnp.concatenate(
                [
                    second[d, p, rows, :],
                    nodes[d, p, rows, :],
                    nodes[d + 1, p, rows, :],
                    second[d + 1, p, rows, :],
                ],
                axis=0,
            )
            for p in range(3)
        ]

    adjoint = [second_adjoint[...], (nodes[1, 0, 24:32, :] + nodes[1, 1, 24:32, :]) + nodes[1, 2, 24:32, :]]
    rows, pair_rows = cycle_terms(
        corner_parts,
        adjoint,
        [scalings[0:1, :], scalings[1:2, :]],
        [scalings[2:3, :], scalings[3:4, :]],
        weights[...],
    )
    pairs[...] = pair_rows

    odd = (lax.axis_index("mer") & 1) == 1
    none = jnp.zeros((1, OWN), f32)

    def four_of_eight(four):
        return jnp.concatenate(
            [jnp.where(odd, 0.0, x) for x in four] + [jnp.where(odd, x, 0.0) for x in four], axis=0
        )

    now = four_of_eight([gradients[0:1, :], rows[0], gradients[1:2, :], rows[1]])
    late = four_of_eight([gradients[2:3, :], rows[2], none, none])
    lower = iota((PAD, WINDOW), 1) < HALF
    fetch.wait()
    start = jnp.int32(0)
    for target in range(GROUPS):
        first = (start >> 4) & (OWN - 1)
        turned = pltpu.roll(now, (OWN - first) & (OWN - 1), 1)
        turned_late = pltpu.roll(late, (OWN + HALF - first) & (OWN - 1), 1)
        sent[target] = jnp.where(lower, turned[:, 0:WINDOW], turned_late[:, 0:WINDOW])
        start = start + counts[0, target]


def load_kernel(first_pairs, second_pairs, order, stress_map, factor, loads, carry):
    stress_rows = jnp.concatenate([stress_map[...], jnp.zeros((5, 24), f32)], axis=0)
    spread_t = corner_rows()
    load_weights = left_stack([matmul_nt(spread_t, part).astype(bf16) for part in parts(stress_rows)], 1)
    lower, upper = [], []
    for pairs in (first_pairs, second_pairs):
        before = matmul(load_weights, right_stack(parts(pairs[0:PAD, :]), 0))
        here = matmul(load_weights, right_stack(parts(pairs[PAD : 2 * PAD, :]), 0))
        lower.append(here[0:8] + before[24:32])
        upper.append(here[8:16] + before[16:24])
    stored = stored_order(jnp.concatenate([lower[0], upper[0] + lower[1], upper[1]], axis=0), order[1])
    stored = factor[0] * stored
    loads[...] = stored[0 : 2 * PAD]
    carry[...] = stored[2 * PAD : 3 * PAD]


def place_kernel(spans, spread_now, spread_late, sources):
    member = lax.axis_index("mer")
    group = iota((1, GROUPS), 1)
    start = jnp.sum(jnp.where(group < member, spans[...], 0), axis=1, keepdims=True)
    count = jnp.sum(jnp.where(group == member, spans[...], 0), axis=1, keepdims=True)
    element = iota((1, MOST), 1) + (start & (GROUPS - 1))
    valid = iota((1, MOST), 1) < count
    for late, spread_ref in ((0, spread_now), (1, spread_late)):
        sources[late : late + 1, :] = jnp.where(valid, (element + late) & (GROUPS - 1), -1)
        third = (iota((HALF, MOST), 0) == ((element + late) >> 4)).astype(f32).astype(bf16)
        for p in range(3):
            spread_ref[p * HALF : (p + 1) * HALF, :] = third


def span_kernel(received, loads, carry, spread_now, spread_late, sources, factor, adjoint_load, thickness_grad):
    values = jnp.concatenate([received[2 * g] + received[2 * g + 1] for g in range(GROUPS // 2)], axis=0)
    lower_half = iota((PAD, MOST), 0) < 4
    both = []
    for late, spread_ref in ((0, spread_now), (1, spread_late)):
        stack = jnp.concatenate(parts(values[:, late * HALF : (late + 1) * HALF]), axis=1)
        rows = matmul(stack, spread_ref[...])
        source = sources[late : late + 1, :]
        wanted = jnp.where(lower_half, source, source - 1)
        picked = jnp.zeros((PAD, MOST), f32)
        for g in range(GROUPS // 2):
            picked = jnp.where(wanted == 2 * g, rows[g * PAD : (g + 1) * PAD], picked)
        both.append(picked[0:4] + picked[4:8])
    thickness_grad[...] = (both[0][0:2] - factor[0] * both[0][2:4]) + both[1][0:2]

    first = loads[0:PAD, :] + carry[...]
    second = loads[PAD : 2 * PAD, :]
    for i in range(DOF):
        adjoint_load[i, 0:1, :] = first[i : i + 1]
        adjoint_load[i, 1:2, :] = second[i : i + 1]


def shape(*dims, dtype=f32):
    return jax.ShapeDtypeStruct(dims, dtype)


def from_behind(block, axis, distance):
    size = lax.axis_size(axis)
    return lax.ppermute(block, axis, [((i - distance) % size, i) for i in range(size)])


def on_device(
    adjoint,
    mode_fields,
    node_slot,
    thickness,
    weld_land,
    panel_spans,
    load_factor,
    membrane,
    bending,
    geometric,
    stress_map,
):
    brought = (stress_map, panel_spans)
    held, held_adjoint, rim, *brought = pl.pallas_call(
        gather_kernel,
        out_shape=(shape(3, 3, DOF, 2, OWN), shape(DOF, 2, OWN), shape(8 * PAD, OWN))
        + tuple(shape(*x.shape, dtype=x.dtype) for x in brought),
        in_specs=[hbm] * (2 + SMALL),
        out_specs=(vmem,) * (3 + SMALL),
        scratch_shapes=[pltpu.SemaphoreType.DMA((4 + SMALL,))],
        compiler_params=small,
    )(*[pltpu.with_memory_space_constraint(x, pltpu.HBM) for x in (mode_fields, adjoint, *brought)])
    stress_map, panel_spans = brought
    rim = from_behind(rim, "circ", -1)
    order, *kept, first_pairs = pl.pallas_call(
        local_kernel,
        out_shape=(
            shape(3, OWN, OWN, dtype=bf16),
            shape(3, 3, 3 * PAD, OWN),
            shape(PAD, OWN),
            shape(176, 192, dtype=bf16),
            shape(PAD, OWN),
            shape(PAD, OWN),
            shape(2 * PAD, OWN),
        ),
        in_specs=[vmem] * 9,
        out_specs=(vmem,) * 7,
        scratch_shapes=[
            pltpu.VMEM((2 * ROWS, LANES), f32),
            pltpu.VMEM((2 * ROWS, LANES), i32),
            pltpu.VMEM((3, 3, 8 * PAD, OWN), f32),
            pltpu.VMEM((3, 8 * PAD, OWN), f32),
        ],
        compiler_params=small,
    )(
        held,
        held_adjoint,
        node_slot.reshape(ROWS, LANES),
        thickness,
        weld_land,
        membrane,
        bending,
        geometric,
        stress_map,
    )
    sent, second_pairs = pl.pallas_call(
        rim_kernel,
        out_shape=(shape(GROUPS, PAD, WINDOW), shape(2 * PAD, OWN)),
        in_specs=[vmem] * 8,
        out_specs=(vmem,) * 2,
        scratch_shapes=[
            pltpu.VMEM((3, 3, 4 * PAD, OWN), f32),
            pltpu.SMEM((1, GROUPS), i32),
            pltpu.SemaphoreType.DMA,
        ],
        compiler_params=small,
    )(rim, order, *kept, panel_spans)
    received = lax.all_to_all(sent, "mer", 0, 0)
    second_pairs, factor = lax.optimization_barrier((second_pairs, load_factor.reshape(1)))
    loads, carry = pl.pallas_call(
        load_kernel,
        out_shape=(shape(2 * PAD, OWN), shape(PAD, OWN)),
        in_specs=[vmem] * 4 + [smem],
        out_specs=(vmem,) * 2,
        compiler_params=small,
    )(first_pairs, second_pairs, order, stress_map, factor)
    carry = from_behind(carry, "circ", 1)
    places = pl.pallas_call(
        place_kernel,
        out_shape=(shape(3 * HALF, MOST, dtype=bf16), shape(3 * HALF, MOST, dtype=bf16), shape(2, MOST, dtype=i32)),
        in_specs=[vmem],
        out_specs=(vmem,) * 3,
        compiler_params=small,
    )(panel_spans)
    return pl.pallas_call(
        span_kernel,
        out_shape=(shape(DOF, 2, OWN), shape(2, MOST)),
        in_specs=[vmem] * 6 + [smem],
        out_specs=(vmem,) * 2,
        compiler_params=small,
    )(received, loads, carry, *places, factor)


def solution(mesh):
    return jax.shard_map(
        on_device,
        mesh=mesh,
        in_specs=(
            P(None, "circ", "mer"),
            P(None, None, "circ", None),
            P(),
            P("circ", None),
            P("circ", None),
            P("circ", None),
            P(),
            P(),
            P(),
            P(),
            P(),
        ),
        out_specs=(P(None, "circ", "mer"), P("circ", "mer")),
        check_vma=False,
    )
```

```python
import jax
import jax.numpy as jnp
from jax import lax
from jax.experimental import pallas as pl
from jax.experimental.pallas import tpu as pltpu
from jax.sharding import PartitionSpec as P


DOF = 6
SMALL = 2
PAD = 8
OWN = 256
GROUPS = 16
COLUMN = OWN * GROUPS
MOST = 768
LANES = 128
ROWS = COLUMN // LANES
WINDOW = 128
HALF = 64

f32, bf16, i32 = jnp.float32, jnp.bfloat16, jnp.int32
vmem = pl.BlockSpec(memory_space=pltpu.VMEM)
smem = pl.BlockSpec(memory_space=pltpu.SMEM)
raw = pl.BlockSpec(memory_space=pl.ANY)
hbm = pl.BlockSpec(memory_space=pltpu.HBM)
small = pltpu.CompilerParams(vmem_limit_bytes=12 << 20)


def iota(shape, axis):
    return lax.broadcasted_iota(i32, shape, axis)


def parts(x):
    high = x.astype(bf16)
    rest = x - high.astype(f32)
    middle = rest.astype(bf16)
    low = (rest - middle.astype(f32)).astype(bf16)
    return high, middle, low


def matmul(a, b):
    return jnp.dot(a, b, preferred_element_type=f32)


def matmul_nt(a, b):
    return lax.dot_general(a, b, (((1,), (1,)), ((), ())), preferred_element_type=f32)


def left_stack(three, axis):
    high, middle, low = three
    return jnp.concatenate([high, high, middle, middle, high, low], axis=axis)


def right_stack(three, axis):
    high, middle, low = three
    return jnp.concatenate([high, middle, high, middle, low, high], axis=axis)


def gather_kernel(modes, adjoint, *rest):
    small_in, rest = rest[:SMALL], rest[SMALL:]
    held, held_adjoint, rim, *rest = rest
    small_out, (sems,) = rest[:SMALL], rest[SMALL:]
    member = lax.axis_index("mer")
    copies = []
    for d in range(3):
        block = (member + (d + GROUPS - 1)) & (GROUPS - 1)
        columns = pl.ds(pl.multiple_of(block * OWN, OWN), OWN)
        copies.append(pltpu.make_async_copy(modes.at[:, :, :, columns], held.at[d], sems.at[d]))
    copies.append(pltpu.make_async_copy(adjoint, held_adjoint, sems.at[3]))
    for i in range(SMALL):
        copies.append(pltpu.make_async_copy(small_in[i], small_out[i], sems.at[4 + i]))
    for copy in copies:
        copy.start()
    rim[56:64, :] = jnp.zeros((PAD, OWN), f32)
    for d in range(3):
        copies[d].wait()
        for f in range(3):
            for i in range(DOF):
                row = (3 * d + f) * DOF + i
                rim[row : row + 1, :] = held[d, f, i, 0:1, :]
    for copy in copies[3:]:
        copy.wait()
    for i in range(DOF):
        rim[54 + i : 55 + i, :] = held_adjoint[i, 0:1, :]


def fold(x):
    return (x[0:8] + x[8:16]) + (x[16:24] + x[24:32])


def column_sum(x):
    return jnp.sum(x, axis=0, keepdims=True)


def pair_terms(corner_parts, d, weights):
    pairs = [jnp.zeros((PAD, OWN), f32)] * 3
    products = []
    for f in range(2):
        three = corner_parts(f, d)
        value = (three[0] + three[1]) + three[2]
        product = matmul(weights, right_stack([t.astype(bf16) for t in three], 0))
        products.append((value, product))
        first = product.shape[0] - 96
        pairs = [
            pairs[s] + fold(value * product[first + 32 * s : first + 32 * s + 32]) for s in range(3)
        ]
    return [column_sum(x) for x in pairs], products


def cycle_terms(corner_parts, adjoint, growth, thick, weights):
    bend = [3.0 * t * t for t in thick]
    pairs, products = pair_terms(corner_parts, 1, weights[0:160])
    stiff = jnp.zeros((PAD, OWN), f32)
    for value, product in products:
        stiff = stiff + fold(value * (product[0:32] + bend[1] * product[32:64]))
    prestate_weights = jnp.concatenate([weights[0:64], weights[160:176]], axis=0)
    here, before = [
        matmul(prestate_weights, right_stack([t.astype(bf16) for t in corner_parts(2, d)], 0))
        for d in (1, 0)
    ]
    tangent = here[0:16] + bend[1] * here[32:48]
    aterm = column_sum(adjoint[0] * tangent[0:8] + adjoint[1] * tangent[8:16])
    coupling = (here[64:65] * pairs[0] + here[65:66] * pairs[1]) + here[66:67] * pairs[2]
    tangent = before[16:32] + bend[0] * before[48:64]
    late_aterm = column_sum(adjoint[0] * tangent[8:16] + adjoint[1] * tangent[0:8])
    rows = [
        growth[1] * (column_sum(stiff) - aterm),
        growth[1] * coupling,
        -(growth[0] * late_aterm),
    ]
    return rows, pairs


def pair_rows(before, here, thick):
    return jnp.concatenate(
        [
            *[thick[0] * x for x in before],
            jnp.zeros((5, OWN), f32),
            *[thick[1] * x for x in here],
            jnp.zeros((5, OWN), f32),
        ],
        axis=0,
    )


def corner_rows():
    entry = iota((32, 24), 1)
    return (iota((32, 24), 0) == (entry // 6) * PAD + entry % 6).astype(f32).astype(bf16)


def stored_order(rows, order):
    n = rows.shape[0]
    placed = matmul_nt(jnp.concatenate(parts(rows), axis=0), order)
    return (placed[0:n] + placed[n : 2 * n]) + placed[2 * n : 3 * n]


def local_kernel(
    held,
    held_adjoint,
    slots,
    thickness,
    weld,
    membrane,
    bending,
    geometric,
    stress_map,
    order,
    second,
    second_adjoint,
    weights,
    scalings,
    gradients,
    pairs,
    thick_rows,
    weld_rows,
    nodes,
    own,
):
    member = lax.axis_index("mer")

    lane = iota((1, OWN), 1)
    position = [(lane * GROUPS + (member + d - 1)) & (COLUMN - 1) for d in range(3)]
    pick = [
        (iota((LANES, OWN), 0) == (position[d] & (LANES - 1))).astype(f32).astype(bf16)
        for d in range(3)
    ]
    for a in range(ROWS):
        thick_rows[2 * a : 2 * a + 2, :] = thickness[:, a * LANES : (a + 1) * LANES]
        weld_rows[2 * a : 2 * a + 2, :] = weld[:, a * LANES : (a + 1) * LANES]
    thick_parts = parts(thick_rows[...])
    weld_part = weld_rows[...].astype(f32).astype(bf16)
    slot_part = (slots[...] & (OWN - 1)).astype(f32).astype(bf16)

    def choose(rows, d, stride, offset):
        here = iota(rows.shape, 0) == (position[d] >> 7) * stride + offset
        return column_sum(jnp.where(here, rows, 0.0))

    growth, thick = {}, {}
    stacked = jnp.concatenate([*thick_parts, weld_part], axis=0)
    for d in range(2):
        rows = matmul(stacked, pick[d])
        thick_all = (rows[0:64] + rows[64:128]) + rows[128:192]
        for r in range(2):
            growth[d, r] = 1.0 + 0.5 * choose(rows[192:256], d, 2, r)
            thick[d, r] = choose(thick_all, d, 2, r) * growth[d, r]
    scalings[...] = jnp.concatenate(
        [growth[0, 1], growth[1, 1], thick[0, 1], thick[1, 1], jnp.zeros((4, OWN), f32)], axis=0
    )

    own[...] = jnp.zeros_like(own)
    for r in range(2):
        for i in range(DOF):
            for d in range(3):
                for f in range(3):
                    row = (f + 3 * r) * PAD + i
                    own[d, row : row + 1, :] = held[d, f, i, r : r + 1, :]
            row = (6 + r) * PAD + i
            own[1, row : row + 1, :] = held_adjoint[i, r : r + 1, :]
    for d in range(3):
        slot = choose(matmul(slot_part, pick[d]), d, 1, 0).astype(i32)
        order[d] = (iota((OWN, OWN), 0) == slot).astype(f32).astype(bf16)
        count = 8 * PAD if d == 1 else 6 * PAD
        values = own[d, 0:count, :]
        placed = matmul(jnp.concatenate(parts(values), axis=0), order[d])
        for p in range(3):
            nodes[d, p, 0:count, :] = placed[p * count : (p + 1) * count]
            second[d, p] = placed[p * count + 24 : p * count + 48]

    spread = (
        iota((24, 32), 1) == (iota((24, 32), 0) // 6) * PAD + iota((24, 32), 0) % 6
    ).astype(f32).astype(bf16)
    spread_t = corner_rows()
    stress_rows = jnp.concatenate([stress_map[...], jnp.zeros((5, 24), f32)], axis=0)
    matrices = [membrane[...], bending[...], geometric[0], geometric[1], geometric[2]]
    pieces = [[], [], []]
    for matrix in matrices:
        for p, part in enumerate(parts(matrix)):
            wide = matmul(part, spread).astype(bf16)
            pieces[p].append(matmul(spread_t, wide))
    for p, part in enumerate(parts(stress_rows)):
        pieces[p].append(matmul(part, spread))
        pieces[p].append(jnp.zeros((PAD, 32), f32))
    weights[...] = left_stack([jnp.concatenate(w, axis=0).astype(bf16) for w in pieces], 1)

    def corner_parts(f, d):
        low, high = f * PAD, (f + 3) * PAD
        return [
            jnp.concatenate(
                [
                    nodes[d, p, low : low + PAD, :],
                    nodes[d, p, high : high + PAD, :],
                    nodes[d + 1, p, high : high + PAD, :],
                    nodes[d + 1, p, low : low + PAD, :],
                ],
                axis=0,
            )
            for p in range(3)
        ]

    adjoint = [
        (nodes[1, 0, g : g + PAD, :] + nodes[1, 1, g : g + PAD, :]) + nodes[1, 2, g : g + PAD, :]
        for g in (48, 56)
    ]
    second_adjoint[...] = adjoint[1]
    thick = [thick[d, 0] for d in range(2)]
    rows, here = cycle_terms(
        corner_parts, adjoint, [growth[d, 0] for d in range(2)], thick, weights[...]
    )
    gradients[...] = jnp.concatenate(rows + [jnp.zeros((5, OWN), f32)], axis=0)
    before, _ = pair_terms(corner_parts, 0, weights[64:160, :])
    pairs[...] = pair_rows(before, here, thick)


def rim_kernel(
    rim,
    order,
    second,
    second_adjoint,
    weights,
    scalings,
    gradients,
    spans,
    sent,
    pairs,
    nodes,
    counts,
    windows,
    sem,
    store_sem,
):
    fetch = pltpu.make_async_copy(spans, counts, sem)
    fetch.start()
    for d in range(3):
        groups = [3 * d, 3 * d + 1, 3 * d + 2] + [9] * (d == 1)
        values = jnp.concatenate([rim[g * DOF : g * DOF + PAD, :] for g in groups], axis=0)
        count = values.shape[0]
        placed = matmul(jnp.concatenate(parts(values), axis=0), order[d])
        for p in range(3):
            nodes[d, p, 0:count, :] = placed[p * count : (p + 1) * count]

    def corner_parts(f, d):
        rows = slice(f * PAD, (f + 1) * PAD)
        return [
            jnp.concatenate(
                [
                    second[d, p, rows, :],
                    nodes[d, p, rows, :],
                    nodes[d + 1, p, rows, :],
                    second[d + 1, p, rows, :],
                ],
                axis=0,
            )
            for p in range(3)
        ]

    adjoint = [second_adjoint[...], (nodes[1, 0, 24:32, :] + nodes[1, 1, 24:32, :]) + nodes[1, 2, 24:32, :]]
    thick = [scalings[2:3, :], scalings[3:4, :]]
    rows, here = cycle_terms(
        corner_parts, adjoint, [scalings[0:1, :], scalings[1:2, :]], thick, weights[...]
    )

    odd = (lax.axis_index("mer") & 1) == 1
    none = jnp.zeros((1, OWN), f32)

    def four_of_eight(four):
        return jnp.concatenate(
            [jnp.where(odd, 0.0, x) for x in four] + [jnp.where(odd, x, 0.0) for x in four], axis=0
        )

    now = four_of_eight([gradients[0:1, :], rows[0], gradients[1:2, :], rows[1]])
    late = four_of_eight([gradients[2:3, :], rows[2], none, none])
    lower = iota((PAD, WINDOW), 1) < HALF
    fetch.wait()
    start = jnp.int32(0)
    for target in range(GROUPS):
        first = (start >> 4) & (OWN - 1)
        turned = pltpu.roll(now, (OWN - first) & (OWN - 1), 1)
        turned_late = pltpu.roll(late, (OWN + HALF - first) & (OWN - 1), 1)
        windows[target] = jnp.where(lower, turned[:, 0:WINDOW], turned_late[:, 0:WINDOW])
        start = start + counts[0, target]
    store = pltpu.make_async_copy(windows, sent, store_sem)
    store.start()
    before, _ = pair_terms(corner_parts, 0, weights[64:160, :])
    pairs[...] = pair_rows(before, here, thick)
    store.wait()


def load_kernel(first_pairs, second_pairs, order, stress_map, factor, loads, carry):
    stress_rows = jnp.concatenate([stress_map[...], jnp.zeros((5, 24), f32)], axis=0)
    spread_t = corner_rows()
    load_weights = left_stack([matmul_nt(spread_t, part).astype(bf16) for part in parts(stress_rows)], 1)
    lower, upper = [], []
    for pairs in (first_pairs, second_pairs):
        before = matmul(load_weights, right_stack(parts(pairs[0:PAD, :]), 0))
        here = matmul(load_weights, right_stack(parts(pairs[PAD : 2 * PAD, :]), 0))
        lower.append(here[0:8] + before[24:32])
        upper.append(here[8:16] + before[16:24])
    stored = stored_order(jnp.concatenate([lower[0], upper[0] + lower[1], upper[1]], axis=0), order[1])
    stored = factor[0] * stored
    loads[...] = stored[0 : 2 * PAD]
    carry[...] = stored[2 * PAD : 3 * PAD]


def place_kernel(spans, spread_now, spread_late, sources):
    member = lax.axis_index("mer")
    group = iota((1, GROUPS), 1)
    start = jnp.sum(jnp.where(group < member, spans[...], 0), axis=1, keepdims=True)
    count = jnp.sum(jnp.where(group == member, spans[...], 0), axis=1, keepdims=True)
    element = iota((1, MOST), 1) + (start & (GROUPS - 1))
    valid = iota((1, MOST), 1) < count
    for late, spread_ref in ((0, spread_now), (1, spread_late)):
        sources[late : late + 1, :] = jnp.where(valid, (element + late) & (GROUPS - 1), -1)
        third = (iota((HALF, MOST), 0) == ((element + late) >> 4)).astype(f32).astype(bf16)
        for p in range(3):
            spread_ref[p * HALF : (p + 1) * HALF, :] = third


def span_kernel(received, loads, carry, spread_now, spread_late, sources, factor, adjoint_load, thickness_grad):
    values = jnp.concatenate([received[2 * g] + received[2 * g + 1] for g in range(GROUPS // 2)], axis=0)
    lower_half = iota((PAD, MOST), 0) < 4
    both = []
    for late, spread_ref in ((0, spread_now), (1, spread_late)):
        stack = jnp.concatenate(parts(values[:, late * HALF : (late + 1) * HALF]), axis=1)
        rows = matmul(stack, spread_ref[...])
        source = sources[late : late + 1, :]
        wanted = jnp.where(lower_half, source, source - 1)
        picked = jnp.zeros((PAD, MOST), f32)
        for g in range(GROUPS // 2):
            picked = jnp.where(wanted == 2 * g, rows[g * PAD : (g + 1) * PAD], picked)
        both.append(picked[0:4] + picked[4:8])
    thickness_grad[...] = (both[0][0:2] - factor[0] * both[0][2:4]) + both[1][0:2]

    first = loads[0:PAD, :] + carry[...]
    second = loads[PAD : 2 * PAD, :]
    for i in range(DOF):
        adjoint_load[i, 0:1, :] = first[i : i + 1]
        adjoint_load[i, 1:2, :] = second[i : i + 1]


def shape(*dims, dtype=f32):
    return jax.ShapeDtypeStruct(dims, dtype)


def from_behind(block, axis, distance):
    size = lax.axis_size(axis)
    return lax.ppermute(block, axis, [((i - distance) % size, i) for i in range(size)])


def on_device(
    adjoint,
    mode_fields,
    node_slot,
    thickness,
    weld_land,
    panel_spans,
    load_factor,
    membrane,
    bending,
    geometric,
    stress_map,
):
    brought = (stress_map, panel_spans)
    held, held_adjoint, rim, *brought = pl.pallas_call(
        gather_kernel,
        out_shape=(shape(3, 3, DOF, 2, OWN), shape(DOF, 2, OWN), shape(8 * PAD, OWN))
        + tuple(shape(*x.shape, dtype=x.dtype) for x in brought),
        in_specs=[hbm] * (2 + SMALL),
        out_specs=(vmem,) * (3 + SMALL),
        scratch_shapes=[pltpu.SemaphoreType.DMA((4 + SMALL,))],
        compiler_params=small,
    )(*[pltpu.with_memory_space_constraint(x, pltpu.HBM) for x in (mode_fields, adjoint, *brought)])
    stress_map, panel_spans = brought
    rim = from_behind(rim, "circ", -1)
    order, *kept, first_pairs = pl.pallas_call(
        local_kernel,
        out_shape=(
            shape(3, OWN, OWN, dtype=bf16),
            shape(3, 3, 3 * PAD, OWN),
            shape(PAD, OWN),
            shape(176, 192, dtype=bf16),
            shape(PAD, OWN),
            shape(PAD, OWN),
            shape(2 * PAD, OWN),
        ),
        in_specs=[vmem] * 9,
        out_specs=(vmem,) * 7,
        scratch_shapes=[
            pltpu.VMEM((2 * ROWS, LANES), f32),
            pltpu.VMEM((2 * ROWS, LANES), i32),
            pltpu.VMEM((3, 3, 8 * PAD, OWN), f32),
            pltpu.VMEM((3, 8 * PAD, OWN), f32),
        ],
        compiler_params=small,
    )(
        held,
        held_adjoint,
        node_slot.reshape(ROWS, LANES),
        thickness,
        weld_land,
        membrane,
        bending,
        geometric,
        stress_map,
    )
    sent, second_pairs = pl.pallas_call(
        rim_kernel,
        out_shape=(shape(GROUPS, PAD, WINDOW), shape(2 * PAD, OWN)),
        in_specs=[vmem] * 8,
        out_specs=(raw, vmem),
        scratch_shapes=[
            pltpu.VMEM((3, 3, 4 * PAD, OWN), f32),
            pltpu.SMEM((1, GROUPS), i32),
            pltpu.VMEM((GROUPS, PAD, WINDOW), f32),
            pltpu.SemaphoreType.DMA,
            pltpu.SemaphoreType.DMA,
        ],
        compiler_params=small,
    )(rim, order, *kept, panel_spans)
    received = lax.all_to_all(sent, "mer", 0, 0)
    second_pairs, factor = lax.optimization_barrier((second_pairs, load_factor.reshape(1)))
    loads, carry = pl.pallas_call(
        load_kernel,
        out_shape=(shape(2 * PAD, OWN), shape(PAD, OWN)),
        in_specs=[vmem] * 4 + [smem],
        out_specs=(vmem,) * 2,
        compiler_params=small,
    )(first_pairs, second_pairs, order, stress_map, factor)
    carry = from_behind(carry, "circ", 1)
    places = pl.pallas_call(
        place_kernel,
        out_shape=(shape(3 * HALF, MOST, dtype=bf16), shape(3 * HALF, MOST, dtype=bf16), shape(2, MOST, dtype=i32)),
        in_specs=[vmem],
        out_specs=(vmem,) * 3,
        compiler_params=small,
    )(panel_spans)
    return pl.pallas_call(
        span_kernel,
        out_shape=(shape(DOF, 2, OWN), shape(2, MOST)),
        in_specs=[vmem] * 6 + [smem],
        out_specs=(vmem,) * 2,
        compiler_params=small,
    )(received, loads, carry, *places, factor)


def solution(mesh):
    return jax.shard_map(
        on_device,
        mesh=mesh,
        in_specs=(
            P(None, "circ", "mer"),
            P(None, None, "circ", None),
            P(),
            P("circ", None),
            P("circ", None),
            P("circ", None),
            P(),
            P(),
            P(),
            P(),
            P(),
        ),
        out_specs=(P(None, "circ", "mer"), P("circ", "mer")),
        check_vma=False,
    )
```
